32 devices in a mesh: row: 4 (over z), col: 4 (over y, core), ch: 2 (over x).
Axes of the slice: x: 2, y: 2, z: 4, core: 2. Of those that a mesh axis runs over, the one named last changes fastest.
Arguments:
- spectra: float32 [384, 128, 1024], P('ch', 'row', 'col'), may hold values from 0 to 1
- pixel_factor: float32 [64, 128, 1024], P(None, 'row', 'col'), may hold values from 0.1 to 1
- channel_factor: float32 [64, 384], P(None, 'ch'), may hold values from 0.1 to 1
- labels: int32 [128, 1024], P('row', 'col'), may hold values from 0 to 3
Outputs:
- smoothed_factor: float32 [64, 128, 1024], P(None, 'row', 'col')
- new_channel: float32 [64, 384], P(None, 'ch')
The draws below stay inside these ranges and needn't reach their ends.
All inputs are finite; a program needn't handle non-finite values.
Results may differ from the reference program's by a relative error of at most 0.000068.
Values sent between devices are 32-bit elements; how exact they have to be, the bound alone decides.
A program may use at most 64 MiB of HBM per device.

```python
import math
import jax
import jax.numpy as jnp
from jax import lax

K = 64
C = 384
SMOOTH = 3
IMG_ROWS = 128
IMG_COLS = 1024


def place_ends(values, own_key, low, top_value):
    index_at = [jax.random.randint(jax.random.fold_in(own_key, axis), (), 0, length) for axis, length in enumerate(values.shape)]
    longest = values.shape.index(max(values.shape))
    beside = index_at[:longest] + [(index_at[longest] + 1) % values.shape[longest]] + index_at[longest + 1:]
    return values.at[tuple(index_at)].set(low).at[tuple(beside)].set(top_value)


def shard_levels(own_key, dims, pieces, low, largest):
    level = 1.0
    for position, parts in pieces:
        draws = jax.random.uniform(jax.random.fold_in(jax.random.fold_in(own_key, 6), position), (parts,), jnp.float32, low / len(pieces), largest / len(pieces))
        level = level * jnp.repeat(jnp.exp(draws), dims[position] // parts).reshape((-1,) + (1,) * (len(dims) - 1 - position))
    return level


def setup_inputs(seed: int = 0) -> dict:
    streams_of = jax.random.split(jax.random.key(seed), 5)
    spectra = jnp.clip(1.0 * jax.random.uniform(streams_of[0], (C, IMG_ROWS, IMG_COLS), jnp.float32) ** shard_levels(streams_of[0], (C, IMG_ROWS, IMG_COLS), ((0, 2), (1, 4), (2, 4)), -0.2, 0.2), 0.0, 1.0)
    pixel_factor = jnp.clip(jnp.exp(math.log(1.0) - 2.3025851 * jax.random.uniform(streams_of[1], (K, IMG_ROWS, IMG_COLS), jnp.float32) ** shard_levels(streams_of[1], (K, IMG_ROWS, IMG_COLS), ((1, 4), (2, 4)), -0.2, 0.2)), 0.1, 1.0)
    channel_factor = jnp.clip(jnp.exp(math.log(1.0) - 2.3025851 * jax.random.uniform(streams_of[2], (K, C), jnp.float32) ** shard_levels(streams_of[2], (K, C), ((1, 2),), -0.2, 0.2)), 0.1, 1.0)
    labels = place_ends(jax.random.randint(streams_of[3], (IMG_ROWS, IMG_COLS), 0, 4), jax.random.fold_in(streams_of[3], 1), 0, 3).astype(jnp.int32)
    return dict(spectra=spectra, pixel_factor=pixel_factor, channel_factor=channel_factor, labels=labels)


epsilon = 1e-9


def coefficients(marked):
    center = marked[1:-1, 1:-1]
    result = []
    for neighbour in (marked[:-2, 1:-1], marked[2:, 1:-1], marked[1:-1, :-2], marked[1:-1, 2:]):
        result.append(jnp.where(neighbour == 0, 0.0, jnp.where(neighbour == center, 1.0, 0.25)).astype(jnp.float32))
    return result


def smooth_once(padded, field, weights):
    combined = field + weights[0] * padded[:, :-2, 1:-1] + weights[1] * padded[:, 2:, 1:-1]
    combined = combined + weights[2] * padded[:, 1:-1, :-2] + weights[3] * padded[:, 1:-1, 2:]
    return combined / (1.0 + weights[0] + weights[1] + weights[2] + weights[3])


def reference(spectra, pixel_factor, channel_factor, labels):
    precise = lax.Precision.HIGHEST
    contraction = (((1,), (1,)), ((), ()))
    factor_rank = pixel_factor.shape[0]
    flat_pixel = pixel_factor.reshape(factor_rank, -1)
    flat_data = spectra.reshape(spectra.shape[0], -1)
    chan_top = lax.dot_general(flat_pixel, flat_data, contraction, precision=precise, preferred_element_type=jnp.float32)
    pixel_gram = lax.dot_general(flat_pixel, flat_pixel, contraction, precision=precise, preferred_element_type=jnp.float32)
    new_channel = channel_factor * chan_top / (jnp.dot(pixel_gram, channel_factor, precision=precise, preferred_element_type=jnp.float32) + epsilon)
    pixel_top = jnp.dot(new_channel, flat_data, precision=precise, preferred_element_type=jnp.float32)
    chan_gram = lax.dot_general(new_channel, new_channel, contraction, precision=precise, preferred_element_type=jnp.float32)
    lower = jnp.dot(chan_gram, flat_pixel, precision=precise, preferred_element_type=jnp.float32)
    raised = (flat_pixel * pixel_top / (lower + epsilon)).reshape(pixel_factor.shape)
    marked = jnp.pad(labels + 1, 1)
    weights = coefficients(marked)
    field = raised
    for iteration in range(SMOOTH):
        padded = jnp.pad(field, ((0, 0), (1, 1), (1, 1)))
        field = smooth_once(padded, field, weights)
    return field, new_channel
```

```python
import functools

import jax
import jax.numpy as jnp
from jax import lax
from jax.experimental import pallas as pl
from jax.experimental.pallas import tpu as pltpu
from jax.sharding import PartitionSpec as P

SMOOTH = 3
MESH = pl.DeviceIdType.MESH
LANES = 128
SUB = 8
CHUNK = 4

epsilon = 1e-09


def split(value):
    high = value.astype(jnp.bfloat16)
    low = (value - high.astype(jnp.float32)).astype(jnp.bfloat16)
    return high, low


def dot(left, right, contraction):
    return lax.dot_general(
        left, right, (contraction, ((), ())), preferred_element_type=jnp.float32
    )


def dot3(left, right, contraction):
    rows = left[0].shape[0]
    both = dot(jnp.concatenate(left, axis=0), right[0], contraction)
    return both[:rows] + both[rows:] + dot(left[0], right[1], contraction)


NT = ((1,), (1,))
NN = ((1,), (0,))


def factor_kernel(
    sizes, x_hbm, w_hbm, cf_ref, lab_ref, field_out, nc_out,
    xw, gram, gram_in, gram_row, nc, part, field, left, right,
    load_sem, g_send, g_recv, z_send, z_recv, n_send, n_recv,
    t_send, t_recv, c_send, c_recv, r_send, r_recv, out_sem,
):
    n_row, n_col, n_ch = sizes
    rank, rows, cols = w_hbm.shape
    chans = x_hbm.shape[0]
    share = rank // n_col
    chunks = rows // CHUNK
    me_row, me_col, me_ch = (lax.axis_index(a) for a in ("row", "col", "ch"))

    def load(r):
        return (
            pltpu.make_async_copy(w_hbm.at[:, r, :], xw.at[r, pl.ds(0, rank), :], load_sem.at[0, r]),
            pltpu.make_async_copy(x_hbm.at[:, r, :], xw.at[r, pl.ds(rank, chans), :], load_sem.at[1, r]),
        )

    for r in range(rows):
        for copy in load(r):
            copy.start()

    barrier = pltpu.get_barrier_semaphore()
    for d in range(1, n_row):
        pl.semaphore_signal(
            barrier, inc=1, device_id={"row": lax.rem(me_row + d, n_row)}, device_id_type=MESH
        )
    for d in range(1, n_col * n_ch):
        pl.semaphore_signal(
            barrier, inc=1, device_id=side(me_col, me_ch, d, n_col, n_ch), device_id_type=MESH
        )

    for buffer in (left, right):
        edge = 0 if buffer is left else n_col - 1

        @pl.when(me_col == edge)
        def _():
            buffer[...] = jnp.zeros_like(buffer)

    for at, edge in ((0, 0), (rows + SMOOTH, n_row - 1)):

        @pl.when(me_row == edge)
        def _():
            field[pl.ds(at, SMOOTH)] = jnp.zeros((SMOOTH,) + field.shape[1:], jnp.float32)

    def marks(r, carry):
        row = (lab_ref[pl.ds(r, 1), :] + 1).astype(jnp.float32)
        field[r + SMOOTH, pl.ds(rank, SUB), pl.ds(0, cols)] = jnp.broadcast_to(row, (SUB, cols))
        return carry

    lax.fori_loop(0, rows, marks, 0)

    gram[...] = jnp.zeros_like(gram)
    for r in range(rows):
        for copy in load(r):
            copy.wait()
        high, low = split(xw[r])
        total = dot3((high[:rank], low[:rank]), (high, low), NT)
        gram[...] += total.reshape(gram.shape)

    pl.semaphore_wait(barrier, n_row - 1 + n_col * n_ch - 1)

    def to_col(d):
        peer = lax.rem(me_col + d, n_col)
        return pltpu.make_async_remote_copy(
            gram.at[peer], gram_in.at[d - 1], g_send.at[d - 1], g_recv.at[d - 1],
            device_id={"col": peer}, device_id_type=MESH,
        )

    for d in range(1, n_col):
        to_col(d).start()
    own = gram[me_col]
    for d in range(1, n_col):
        to_col(d).wait_recv()
        own = own + gram_in[d - 1]
    gram_row[me_row] = own

    def to_row(d):
        peer = lax.rem(me_row + d, n_row)
        return pltpu.make_async_remote_copy(
            gram_row.at[me_row], gram_row.at[me_row], z_send.at[d - 1], z_recv.at[d - 1],
            device_id={"row": peer}, device_id_type=MESH,
        )

    def from_row(d):
        peer = lax.rem(me_row + n_row - d, n_row)
        return pltpu.make_async_remote_copy(
            gram_row.at[peer], gram_row.at[peer], z_send.at[d - 1], z_recv.at[d - 1],
            device_id={"row": peer}, device_id_type=MESH,
        )

    for d in range(1, n_row):
        to_row(d).start()
    for d in range(1, n_row):
        from_row(d).wait_recv()
    total = gram_row[0]
    for z in range(1, n_row):
        total = total + gram_row[z]
    lower = jnp.dot(
        total[:, :rank], cf_ref[...], precision=lax.Precision.HIGHEST,
        preferred_element_type=jnp.float32,
    )
    own_cf = cf_ref[pl.ds(pl.multiple_of(me_col * share, share), share), :]
    nc[me_ch, me_col] = own_cf * total[:, rank:] / (lower + epsilon)

    def to_side(d):
        return pltpu.make_async_remote_copy(
            nc.at[me_ch, me_col], nc.at[me_ch, me_col], n_send.at[d - 1], n_recv.at[d - 1],
            device_id=side(me_col, me_ch, d, n_col, n_ch), device_id_type=MESH,
        )

    def from_side(d):
        at = side(me_col, me_ch, n_col * n_ch - d, n_col, n_ch)
        slot = nc.at[at["ch"], at["col"]]
        return pltpu.make_async_remote_copy(
            slot, slot, n_send.at[d - 1], n_recv.at[d - 1],
            device_id=at, device_id_type=MESH,
        )

    for d in range(1, n_col * n_ch):
        to_side(d).start()
    for d in range(1, n_col * n_ch):
        from_side(d).wait_recv()

    mine = nc[me_ch].reshape(rank, chans)
    nc_out[...] = mine
    mine = split(mine)

    def chunk_of(i):
        return lax.rem(i + chunks - 1, chunks)

    def to_ch(d, c):
        peer = lax.rem(me_ch + d, n_ch)
        slot = part.at[me_ch, pl.ds(c * CHUNK, CHUNK)]
        return pltpu.make_async_remote_copy(
            slot, slot, t_send.at[d - 1, c], t_recv.at[d - 1, c],
            device_id={"ch": peer}, device_id_type=MESH,
        )

    def from_ch(d, c):
        peer = lax.rem(me_ch + n_ch - d, n_ch)
        slot = part.at[peer, pl.ds(c * CHUNK, CHUNK)]
        return pltpu.make_async_remote_copy(
            slot, slot, t_send.at[d - 1, c], t_recv.at[d - 1, c],
            device_id={"ch": peer}, device_id_type=MESH,
        )

    def send_part(i, carry):
        c = chunk_of(i)
        for k in range(CHUNK):
            r = c * CHUNK + k
            part[me_ch, r] = dot3(mine, split(xw[r, pl.ds(rank, chans), :]), NN)
        for d in range(1, n_ch):
            to_ch(d, c).start()
        return carry

    lax.fori_loop(0, chunks, send_part, 0)

    cg = jnp.zeros((rank, rank), jnp.float32)
    for h in range(n_ch):
        block = nc[h].reshape(rank, chans)
        cg = cg + lax.dot_general(
            block, block, (NT, ((), ())), precision=lax.Precision.HIGHEST,
            preferred_element_type=jnp.float32,
        )
    cg = split(cg)

    def to_right(c):
        return pltpu.make_async_remote_copy(
            field.at[pl.ds(c * CHUNK + SMOOTH, CHUNK), :, pl.ds(cols - LANES, LANES)],
            left.at[pl.ds(c * CHUNK, CHUNK)], c_send.at[0, c], c_recv.at[0, c],
            device_id={"col": lax.rem(me_col + 1, n_col)}, device_id_type=MESH,
        )

    def to_left(c):
        return pltpu.make_async_remote_copy(
            field.at[pl.ds(c * CHUNK + SMOOTH, CHUNK), :, pl.ds(0, LANES)],
            right.at[pl.ds(c * CHUNK, CHUNK)], c_send.at[1, c], c_recv.at[1, c],
            device_id={"col": lax.rem(me_col + n_col - 1, n_col)}, device_id_type=MESH,
        )

    def raise_chunk(i):
        c = chunk_of(i)
        for d in range(1, n_ch):
            from_ch(d, c).wait_recv()
        for k in range(CHUNK):
            r = c * CHUNK + k
            w = xw[r, pl.ds(0, rank), :]
            top = part[0, r]
            for h in range(1, n_ch):
                top = top + part[h, r]
            low = dot3(cg, split(w), NN)
            field[r + SMOOTH, pl.ds(0, rank), pl.ds(0, cols)] = w * top / (low + epsilon)

        @pl.when(me_col < n_col - 1)
        def _():
            to_right(c).start()

        @pl.when(me_col > 0)
        def _():
            to_left(c).start()

    lane = lax.broadcasted_iota(jnp.int32, (CHUNK, rank + SUB, LANES), 2)

    def widen_chunk(i):
        c = chunk_of(i)

        @pl.when(me_col > 0)
        def _():
            to_right(c).wait_recv()

        @pl.when(me_col < n_col - 1)
        def _():
            to_left(c).wait_recv()

        from_right = jnp.where(lane < SMOOTH, right[pl.ds(c * CHUNK, CHUNK)], 0.0)
        wide = jnp.where(lane >= LANES - SMOOTH, left[pl.ds(c * CHUNK, CHUNK)], from_right)
        field[pl.ds(c * CHUNK + SMOOTH, CHUNK), :, pl.ds(cols, LANES)] = wide

    def to_down():
        return pltpu.make_async_remote_copy(
            field.at[pl.ds(rows, SMOOTH)], field.at[pl.ds(0, SMOOTH)], r_send.at[0], r_recv.at[0],
            device_id={"row": lax.rem(me_row + 1, n_row)}, device_id_type=MESH,
        )

    def to_up():
        return pltpu.make_async_remote_copy(
            field.at[pl.ds(SMOOTH, SMOOTH)], field.at[pl.ds(rows + SMOOTH, SMOOTH)],
            r_send.at[1], r_recv.at[1],
            device_id={"row": lax.rem(me_row + n_row - 1, n_row)}, device_id_type=MESH,
        )

    raise_chunk(0)
    raise_chunk(1)
    widen_chunk(0)
    raise_chunk(2)
    widen_chunk(1)

    @pl.when(me_row < n_row - 1)
    def _():
        to_down().start()

    @pl.when(me_row > 0)
    def _():
        to_up().start()

    def step(i, carry):
        raise_chunk(i)
        widen_chunk(i - 1)
        return carry

    lax.fori_loop(3, chunks, step, 0)
    widen_chunk(chunks - 1)

    @pl.when(me_row > 0)
    def _():
        to_down().wait_recv()

    @pl.when(me_row < n_row - 1)
    def _():
        to_up().wait_recv()

    out = pltpu.make_async_copy(field, field_out, out_sem)
    out.start()

    for d in range(1, n_col):
        to_col(d).wait_send()
    for d in range(1, n_row):
        to_row(d).wait_send()
    for d in range(1, n_col * n_ch):
        to_side(d).wait_send()

    def drain(c, carry):
        for d in range(1, n_ch):
            to_ch(d, c).wait_send()

        @pl.when(me_col < n_col - 1)
        def _():
            to_right(c).wait_send()

        @pl.when(me_col > 0)
        def _():
            to_left(c).wait_send()

        return carry

    lax.fori_loop(0, chunks, drain, 0)

    @pl.when(me_row < n_row - 1)
    def _():
        to_down().wait_send()

    @pl.when(me_row > 0)
    def _():
        to_up().wait_send()

    out.wait()


def side(me_col, me_ch, d, n_col, n_ch):
    place = lax.rem(me_col * n_ch + me_ch + d, n_col * n_ch)
    return {"col": place // n_ch, "ch": lax.rem(place, n_ch)}


def smooth_kernel(field_ref, out_hbm, weight, first, second, done, out_sem):
    rank, rows, cols = out_hbm.shape
    wide = field_ref.shape[2]
    groups = rank // SUB

    def coefficients(e, carry):
        center = field_ref[e, pl.ds(rank, SUB), :]
        around = (
            field_ref[e - 1, pl.ds(rank, SUB), :],
            field_ref[e + 1, pl.ds(rank, SUB), :],
            pltpu.roll(center, 1, 1),
            pltpu.roll(center, wide - 1, 1),
        )
        parts = [
            jnp.where(near == 0, 0.0, jnp.where(near == center, 1.0, 0.25)) for near in around
        ]
        scale = 1.0 / (1.0 + parts[0] + parts[1] + parts[2] + parts[3])
        weight[e, 0] = scale
        for j in range(4):
            weight[e, j + 1] = parts[j] * scale
        return carry

    lax.fori_loop(1, rows + 2 * SMOOTH - 1, coefficients, 0)

    def smooth(source, e):
        here = source[e, pl.ds(0, rank), :].reshape(groups, SUB, wide)
        up = source[e - 1, pl.ds(0, rank), :].reshape(groups, SUB, wide)
        down = source[e + 1, pl.ds(0, rank), :].reshape(groups, SUB, wide)
        total = weight[e, 0] * here + weight[e, 1] * up + weight[e, 2] * down
        total = total + weight[e, 3] * pltpu.roll(here, 1, 2)
        total = total + weight[e, 4] * pltpu.roll(here, wide - 1, 2)
        return total.reshape(rank, wide)

    def one(e, carry):
        first[e] = smooth(field_ref, e)
        return carry

    def two(e, carry):
        second[e] = smooth(first, e)
        return carry

    def put(r):
        return pltpu.make_async_copy(done.at[r], out_hbm.at[:, r, :], out_sem.at[r])

    lax.fori_loop(1, rows + 5, one, 0)
    lax.fori_loop(2, rows + 4, two, 0)
    for r in range(rows):
        done[r] = smooth(second, r + SMOOTH)[:, :cols]
        put(r).start()
    for r in range(rows):
        put(r).wait()


def shards(sizes, spectra, pixel_factor, channel_factor, labels):
    n_row, n_col, n_ch = sizes
    rank, rows, cols = pixel_factor.shape
    chans = spectra.shape[0]
    share = rank // n_col
    chunks = rows // CHUNK
    tall = rows + 2 * SMOOTH
    wide = cols + LANES
    f32 = jnp.float32
    vmem = pl.BlockSpec(memory_space=pltpu.VMEM)
    anywhere = pl.BlockSpec(memory_space=pl.ANY)
    dma = pltpu.SemaphoreType.DMA
    field, new_channel = pl.pallas_call(
        functools.partial(factor_kernel, sizes),
        out_shape=(
            jax.ShapeDtypeStruct((tall, rank + SUB, wide), f32),
            jax.ShapeDtypeStruct(channel_factor.shape, f32),
        ),
        in_specs=[anywhere, anywhere, vmem, vmem],
        out_specs=(anywhere, vmem),
        scratch_shapes=[
            pltpu.VMEM((rows, rank + chans, cols), f32),
            pltpu.VMEM((n_col, share, rank + chans), f32),
            pltpu.VMEM((n_col - 1, share, rank + chans), f32),
            pltpu.VMEM((n_row, share, rank + chans), f32),
            pltpu.VMEM((n_ch, n_col, share, chans), f32),
            pltpu.VMEM((n_ch, rows, rank, cols), f32),
            pltpu.VMEM((tall, rank + SUB, wide), f32),
            pltpu.VMEM((rows, rank + SUB, LANES), f32),
            pltpu.VMEM((rows, rank + SUB, LANES), f32),
            dma((2, rows)),
            dma((n_col - 1,)), dma((n_col - 1,)),
            dma((n_row - 1,)), dma((n_row - 1,)),
            dma((n_col * n_ch - 1,)), dma((n_col * n_ch - 1,)),
            dma((n_ch - 1, chunks)), dma((n_ch - 1, chunks)),
            dma((2, chunks)), dma((2, chunks)),
            dma((2,)), dma((2,)),
            dma,
        ],
        compiler_params=pltpu.CompilerParams(
            collective_id=0, has_side_effects=True, vmem_limit_bytes=60 * 1024 * 1024
        ),
        name="factor",
    )(spectra, pixel_factor, channel_factor, labels)
    smoothed = pl.pallas_call(
        smooth_kernel,
        out_shape=jax.ShapeDtypeStruct(pixel_factor.shape, f32),
        in_specs=[vmem],
        out_specs=anywhere,
        scratch_shapes=[
            pltpu.VMEM((tall, 5, SUB, wide), f32),
            pltpu.VMEM((tall, rank, wide), f32),
            pltpu.VMEM((tall, rank, wide), f32),
            pltpu.VMEM((rows, rank, cols), f32),
            dma((rows,)),
        ],
        compiler_params=pltpu.CompilerParams(vmem_limit_bytes=48 * 1024 * 1024),
        name="smooth",
    )(field)
    return smoothed, new_channel


def solution(mesh):
    sizes = tuple(mesh.shape[a] for a in ("row", "col", "ch"))
    placed = (P("ch", "row", "col"), P(None, "row", "col"), P(None, "ch"), P("row", "col"))
    return jax.shard_map(
        functools.partial(shards, sizes),
        mesh=mesh,
        in_specs=placed,
        out_specs=(P(None, "row", "col"), P(None, "ch")),
        check_vma=False,
    )
```

```python
import functools

import jax
import jax.numpy as jnp
from jax import lax
from jax.experimental import pallas as pl
from jax.experimental.pallas import tpu as pltpu
from jax.sharding import PartitionSpec as P

SMOOTH = 3
MESH = pl.DeviceIdType.MESH
LANES = 128
SUB = 8
CHUNK = 2
EDGE = -(-SMOOTH // CHUNK)
LAG = 3

epsilon = 1e-09


def split(value):
    high = value.astype(jnp.bfloat16)
    low = (value - high.astype(jnp.float32)).astype(jnp.bfloat16)
    return high, low


def dot(left, right, contraction):
    return lax.dot_general(
        left, right, (contraction, ((), ())), preferred_element_type=jnp.float32
    )


def dot3(left, right, contraction):
    rows = left[0].shape[0]
    both = dot(jnp.concatenate(left, axis=0), right[0], contraction)
    return both[:rows] + both[rows:] + dot(left[0], right[1], contraction)


NT = ((1,), (1,))
NN = ((1,), (0,))


def factor_kernel(
    sizes, x_hbm, w_hbm, cf_ref, lab_ref, out_hbm, nc_out,
    xw, other, gram, gram_in, gram_row, nc, part, field, left, right, weight, first, second, done,
    load_sem, e_send, e_recv, g_send, g_recv, z_send, z_recv, n_send, n_recv,
    t_send, t_recv, c_send, c_recv, r_send, r_recv, out_sem,
):
    n_row, n_col, n_ch = sizes
    rank, rows, cols = w_hbm.shape
    chans = x_hbm.shape[0]
    share = rank // n_col
    chunks = rows // CHUNK
    early = rows - EDGE * CHUNK
    wide = cols + LANES
    me_row, me_col, me_ch = (lax.axis_index(a) for a in ("row", "col", "ch"))

    def load(r):
        return (
            pltpu.make_async_copy(w_hbm.at[:, r, :], xw.at[r, pl.ds(0, rank), :], load_sem.at[0, r]),
            pltpu.make_async_copy(x_hbm.at[:, r, :], xw.at[r, pl.ds(rank, chans), :], load_sem.at[1, r]),
        )

    order = tuple(range(early, rows)) + tuple(range(early))
    for r in order:
        for copy in load(r):
            copy.start()

    barrier = pltpu.get_barrier_semaphore()
    for d in range(1, n_row):
        pl.semaphore_signal(
            barrier, inc=1, device_id={"row": lax.rem(me_row + d, n_row)}, device_id_type=MESH
        )
    for d in range(1, n_col * n_ch):
        pl.semaphore_signal(
            barrier, inc=1, device_id=side(me_col, me_ch, d, n_col, n_ch), device_id_type=MESH
        )

    for buffer in (left, right):
        edge = 0 if buffer is left else n_col - 1

        @pl.when(me_col == edge)
        def _():
            buffer[...] = jnp.zeros_like(buffer)

    for at, edge in ((0, 0), (rows + SMOOTH, n_row - 1)):

        @pl.when(me_row == edge)
        def _():
            field[pl.ds(at, SMOOTH)] = jnp.zeros((SMOOTH,) + field.shape[1:], jnp.float32)

    def marks(r, carry):
        row = (lab_ref[pl.ds(r, 1), :] + 1).astype(jnp.float32)
        field[r + SMOOTH, pl.ds(rank, SUB), pl.ds(0, cols)] = jnp.broadcast_to(row, (SUB, cols))
        return carry

    lax.fori_loop(0, rows, marks, 0)

    gram[...] = jnp.zeros_like(gram)

    def to_early(d):
        return pltpu.make_async_remote_copy(
            xw.at[pl.ds(early, rows - early), pl.ds(rank, chans), :], other.at[d - 1],
            e_send.at[d - 1], e_recv.at[d - 1],
            device_id={"ch": lax.rem(me_ch + d, n_ch)}, device_id_type=MESH,
        )

    for r in order[: rows - early]:
        for copy in load(r):
            copy.wait()
    pl.semaphore_wait(barrier, n_row - 1 + n_col * n_ch - 1)
    for d in range(1, n_ch):
        to_early(d).start()
    for i, r in enumerate(order):
        if i >= rows - early:
            for copy in load(r):
                copy.wait()
        high, low = split(xw[r])
        total = dot3((high[:rank], low[:rank]), (high, low), NT)
        gram[...] += total.reshape(gram.shape)

    def to_col(d):
        peer = lax.rem(me_col + d, n_col)
        return pltpu.make_async_remote_copy(
            gram.at[peer], gram_in.at[d - 1], g_send.at[d - 1], g_recv.at[d - 1],
            device_id={"col": peer}, device_id_type=MESH,
        )

    for d in range(1, n_col):
        to_col(d).start()
    own = gram[me_col]
    for d in range(1, n_col):
        to_col(d).wait_recv()
        own = own + gram_in[d - 1]
    gram_row[me_row] = own

    def to_row(d):
        peer = lax.rem(me_row + d, n_row)
        return pltpu.make_async_remote_copy(
            gram_row.at[me_row], gram_row.at[me_row], z_send.at[d - 1], z_recv.at[d - 1],
            device_id={"row": peer}, device_id_type=MESH,
        )

    def from_row(d):
        peer = lax.rem(me_row + n_row - d, n_row)
        return pltpu.make_async_remote_copy(
            gram_row.at[peer], gram_row.at[peer], z_send.at[d - 1], z_recv.at[d - 1],
            device_id={"row": peer}, device_id_type=MESH,
        )

    for d in range(1, n_row):
        to_row(d).start()
    for d in range(1, n_row):
        from_row(d).wait_recv()
    total = gram_row[0]
    for z in range(1, n_row):
        total = total + gram_row[z]
    lower = jnp.dot(
        total[:, :rank], cf_ref[...], precision=lax.Precision.HIGHEST,
        preferred_element_type=jnp.float32,
    )
    own_cf = cf_ref[pl.ds(pl.multiple_of(me_col * share, share), share), :]
    nc[me_ch, me_col] = own_cf * total[:, rank:] / (lower + epsilon)

    def to_side(d):
        return pltpu.make_async_remote_copy(
            nc.at[me_ch, me_col], nc.at[me_ch, me_col], n_send.at[d - 1], n_recv.at[d - 1],
            device_id=side(me_col, me_ch, d, n_col, n_ch), device_id_type=MESH,
        )

    def from_side(d):
        at = side(me_col, me_ch, n_col * n_ch - d, n_col, n_ch)
        slot = nc.at[at["ch"], at["col"]]
        return pltpu.make_async_remote_copy(
            slot, slot, n_send.at[d - 1], n_recv.at[d - 1],
            device_id=at, device_id_type=MESH,
        )

    for d in range(1, n_col * n_ch):
        to_side(d).start()
    for d in range(1, n_col * n_ch):
        from_side(d).wait_recv()

    mine = nc[me_ch].reshape(rank, chans)
    nc_out[...] = mine
    mine = split(mine)

    def chunk_of(i):
        return lax.rem(i + chunks - EDGE, chunks)

    def to_ch(d, c):
        peer = lax.rem(me_ch + d, n_ch)
        slot = part.at[me_ch, pl.ds(c * CHUNK, CHUNK)]
        return pltpu.make_async_remote_copy(
            slot, slot, t_send.at[d - 1, c], t_recv.at[d - 1, c],
            device_id={"ch": peer}, device_id_type=MESH,
        )

    def from_ch(d, c):
        peer = lax.rem(me_ch + n_ch - d, n_ch)
        slot = part.at[peer, pl.ds(c * CHUNK, CHUNK)]
        return pltpu.make_async_remote_copy(
            slot, slot, t_send.at[d - 1, c], t_recv.at[d - 1, c],
            device_id={"ch": peer}, device_id_type=MESH,
        )

    def send_part(i, carry):
        c = chunk_of(i)
        for k in range(CHUNK):
            r = c * CHUNK + k
            part[me_ch, r] = dot3(mine, split(xw[r, pl.ds(rank, chans), :]), NN)
        for d in range(1, n_ch):
            to_ch(d, c).start()
        return carry

    lax.fori_loop(EDGE, chunks, send_part, 0)

    for r in range(early, rows):
        part[me_ch, r] = dot3(mine, split(xw[r, pl.ds(rank, chans), :]), NN)
    for d in range(1, n_ch):
        peer = lax.rem(me_ch + n_ch - d, n_ch)
        theirs = split(nc[peer].reshape(rank, chans))
        to_early(d).wait_recv()
        for r in range(early, rows):
            part[peer, r] = dot3(theirs, split(other[d - 1, r - early]), NN)

    cg = jnp.zeros((rank, rank), jnp.float32)
    for h in range(n_ch):
        block = nc[h].reshape(rank, chans)
        cg = cg + lax.dot_general(
            block, block, (NT, ((), ())), precision=lax.Precision.HIGHEST,
            preferred_element_type=jnp.float32,
        )
    cg = split(cg)

    def to_right(c):
        return pltpu.make_async_remote_copy(
            field.at[pl.ds(c * CHUNK + SMOOTH, CHUNK), :, pl.ds(cols - LANES, LANES)],
            left.at[pl.ds(c * CHUNK, CHUNK)], c_send.at[0, c], c_recv.at[0, c],
            device_id={"col": lax.rem(me_col + 1, n_col)}, device_id_type=MESH,
        )

    def to_left(c):
        return pltpu.make_async_remote_copy(
            field.at[pl.ds(c * CHUNK + SMOOTH, CHUNK), :, pl.ds(0, LANES)],
            right.at[pl.ds(c * CHUNK, CHUNK)], c_send.at[1, c], c_recv.at[1, c],
            device_id={"col": lax.rem(me_col + n_col - 1, n_col)}, device_id_type=MESH,
        )

    def raise_chunk(i, awaited=True):
        c = chunk_of(i)
        if awaited:
            for d in range(1, n_ch):
                from_ch(d, c).wait_recv()
        for k in range(CHUNK):
            r = c * CHUNK + k
            w = xw[r, pl.ds(0, rank), :]
            top = part[0, r]
            for h in range(1, n_ch):
                top = top + part[h, r]
            low = dot3(cg, split(w), NN)
            field[r + SMOOTH, pl.ds(0, rank), pl.ds(0, cols)] = w * top / (low + epsilon)

        @pl.when(me_col < n_col - 1)
        def _():
            to_right(c).start()

        @pl.when(me_col > 0)
        def _():
            to_left(c).start()

    lane = lax.broadcasted_iota(jnp.int32, (CHUNK, rank + SUB, LANES), 2)

    def widen_chunk(i):
        c = chunk_of(i)

        @pl.when(me_col > 0)
        def _():
            to_right(c).wait_recv()

        @pl.when(me_col < n_col - 1)
        def _():
            to_left(c).wait_recv()

        from_right = jnp.where(lane < SMOOTH, right[pl.ds(c * CHUNK, CHUNK)], 0.0)
        wide = jnp.where(lane >= LANES - SMOOTH, left[pl.ds(c * CHUNK, CHUNK)], from_right)
        field[pl.ds(c * CHUNK + SMOOTH, CHUNK), :, pl.ds(cols, LANES)] = wide

    def to_down():
        return pltpu.make_async_remote_copy(
            field.at[pl.ds(rows, SMOOTH)], field.at[pl.ds(0, SMOOTH)], r_send.at[0], r_recv.at[0],
            device_id={"row": lax.rem(me_row + 1, n_row)}, device_id_type=MESH,
        )

    def to_up():
        return pltpu.make_async_remote_copy(
            field.at[pl.ds(SMOOTH, SMOOTH)], field.at[pl.ds(rows + SMOOTH, SMOOTH)],
            r_send.at[1], r_recv.at[1],
            device_id={"row": lax.rem(me_row + n_row - 1, n_row)}, device_id_type=MESH,
        )

    def coefficients(e):
        center = field[e, pl.ds(rank, SUB), :]
        around = (
            field[e - 1, pl.ds(rank, SUB), :],
            field[e + 1, pl.ds(rank, SUB), :],
            pltpu.roll(center, 1, 1),
            pltpu.roll(center, wide - 1, 1),
        )
        parts = [
            jnp.where(near == 0, 0.0, jnp.where(near == center, 1.0, 0.25)) for near in around
        ]
        scale = 1.0 / (1.0 + parts[0] + parts[1] + parts[2] + parts[3])
        weight[e, 0] = scale
        for j in range(4):
            weight[e, j + 1] = parts[j] * scale

    def smooth(source, e):
        here, up, down = (
            source[at, pl.ds(0, rank), :].reshape(rank // SUB, SUB, wide)
            for at in (e, e - 1, e + 1)
        )
        total = weight[e, 0] * here + weight[e, 1] * up + weight[e, 2] * down
        total = total + weight[e, 3] * pltpu.roll(here, 1, 2)
        total = total + weight[e, 4] * pltpu.roll(here, wide - 1, 2)
        return total.reshape(rank, wide)

    def put(r):
        return pltpu.make_async_copy(done.at[r], out_hbm.at[:, r, :], out_sem.at[r])

    def one(e, carry):
        coefficients(e)
        first[e] = smooth(field, e)
        return carry

    def two(e, carry):
        second[e] = smooth(first, e)
        return carry

    def three(e, carry):
        done[e - SMOOTH] = smooth(second, e)[:, :cols]
        put(e - SMOOTH).start()
        return carry

    def sweep(starts, counts):
        for stage, start, count in zip((one, two, three), starts, counts):
            lax.fori_loop(0, count, lambda k, v, f=stage, s=start: f(s + k, v), 0)

    def sweep_chunk(c):
        sweep((CHUNK * c + 2, CHUNK * c + 1, CHUNK * c), (CHUNK,) * 3)

    for i in range(2 * EDGE):
        raise_chunk(i, awaited=i >= EDGE)
    for i in range(2 * EDGE):
        widen_chunk(i)

    @pl.when(me_row < n_row - 1)
    def _():
        to_down().start()

    @pl.when(me_row > 0)
    def _():
        to_up().start()

    for i in range(2 * EDGE, 2 * EDGE + LAG):
        raise_chunk(i)
        if i > 2 * EDGE:
            widen_chunk(i - 1)

    @pl.when(me_row > 0)
    def _():
        to_down().wait_recv()

    @pl.when(me_row < n_row - 1)
    def _():
        to_up().wait_recv()

    tip = CHUNK * EDGE
    sweep((1, 2, 3), (tip + 1, tip - 1, tip - 3))
    for c in range(EDGE, EDGE + LAG - 1):
        sweep_chunk(c)

    def step(i, carry):
        raise_chunk(i)
        widen_chunk(i - 1)
        sweep_chunk(i - 1 - EDGE)
        return carry

    lax.fori_loop(2 * EDGE + LAG, chunks, step, 0)
    widen_chunk(chunks - 1)
    sweep_chunk(chunks - 1 - EDGE)
    sweep((early + 2, early + 1, early), (tip + 3,) * 3)

    for d in range(1, n_col):
        to_col(d).wait_send()
    for d in range(1, n_row):
        to_row(d).wait_send()
    for d in range(1, n_col * n_ch):
        to_side(d).wait_send()

    def drain(c, carry):
        @pl.when(me_col < n_col - 1)
        def _():
            to_right(c).wait_send()

        @pl.when(me_col > 0)
        def _():
            to_left(c).wait_send()

        return carry

    lax.fori_loop(0, chunks, drain, 0)

    def drain_part(i, carry):
        for d in range(1, n_ch):
            to_ch(d, chunk_of(i)).wait_send()
        return carry

    lax.fori_loop(EDGE, chunks, drain_part, 0)
    for d in range(1, n_ch):
        to_early(d).wait_send()

    @pl.when(me_row < n_row - 1)
    def _():
        to_down().wait_send()

    @pl.when(me_row > 0)
    def _():
        to_up().wait_send()

    def drain_out(r, carry):
        put(r).wait()
        return carry

    lax.fori_loop(0, rows, drain_out, 0)


def side(me_col, me_ch, d, n_col, n_ch):
    place = lax.rem(me_col * n_ch + me_ch + d, n_col * n_ch)
    return {"col": place // n_ch, "ch": lax.rem(place, n_ch)}


def shards(sizes, spectra, pixel_factor, channel_factor, labels):
    n_row, n_col, n_ch = sizes
    rank, rows, cols = pixel_factor.shape
    chans = spectra.shape[0]
    share = rank // n_col
    chunks = rows // CHUNK
    tall = rows + 2 * SMOOTH
    wide = cols + LANES
    f32 = jnp.float32
    vmem = pl.BlockSpec(memory_space=pltpu.VMEM)
    anywhere = pl.BlockSpec(memory_space=pl.ANY)
    dma = pltpu.SemaphoreType.DMA
    return pl.pallas_call(
        functools.partial(factor_kernel, sizes),
        out_shape=(
            jax.ShapeDtypeStruct(pixel_factor.shape, f32),
            jax.ShapeDtypeStruct(channel_factor.shape, f32),
        ),
        in_specs=[anywhere, anywhere, vmem, vmem],
        out_specs=(anywhere, vmem),
        scratch_shapes=[
            pltpu.VMEM((rows, rank + chans, cols), f32),
            pltpu.VMEM((n_ch - 1, EDGE * CHUNK, chans, cols), f32),
            pltpu.VMEM((n_col, share, rank + chans), f32),
            pltpu.VMEM((n_col - 1, share, rank + chans), f32),
            pltpu.VMEM((n_row, share, rank + chans), f32),
            pltpu.VMEM((n_ch, n_col, share, chans), f32),
            pltpu.VMEM((n_ch, rows, rank, cols), f32),
            pltpu.VMEM((tall, rank + SUB, wide), f32),
            pltpu.VMEM((rows, rank + SUB, LANES), f32),
            pltpu.VMEM((rows, rank + SUB, LANES), f32),
            pltpu.VMEM((tall, 5, SUB, wide), f32),
            pltpu.VMEM((tall, rank, wide), f32),
            pltpu.VMEM((tall, rank, wide), f32),
            pltpu.VMEM((rows, rank, cols), f32),
            dma((2, rows)),
            dma((n_ch - 1,)), dma((n_ch - 1,)),
            dma((n_col - 1,)), dma((n_col - 1,)),
            dma((n_row - 1,)), dma((n_row - 1,)),
            dma((n_col * n_ch - 1,)), dma((n_col * n_ch - 1,)),
            dma((n_ch - 1, chunks)), dma((n_ch - 1, chunks)),
            dma((2, chunks)), dma((2, chunks)),
            dma((2,)), dma((2,)),
            dma((rows,)),
        ],
        compiler_params=pltpu.CompilerParams(
            collective_id=0, has_side_effects=True, vmem_limit_bytes=60 * 1024 * 1024
        ),
        name="factor",
    )(spectra, pixel_factor, channel_factor, labels)


def solution(mesh):
    sizes = tuple(mesh.shape[a] for a in ("row", "col", "ch"))
    placed = (P("ch", "row", "col"), P(None, "row", "col"), P(None, "ch"), P("row", "col"))
    return jax.shard_map(
        functools.partial(shards, sizes),
        mesh=mesh,
        in_specs=placed,
        out_specs=(P(None, "row", "col"), P(None, "ch")),
        check_vma=False,
    )
```

```python
import functools

import jax
import jax.numpy as jnp
from jax import lax
from jax.experimental import pallas as pl
from jax.experimental.pallas import tpu as pltpu
from jax.sharding import PartitionSpec as P

SMOOTH = 3
MESH = pl.DeviceIdType.MESH
LANES = 128
SUB = 8
CHUNK = 2
EDGE = -(-SMOOTH // CHUNK)
LAG = 3

epsilon = 1e-09


def split(value):
    high = value.astype(jnp.bfloat16)
    low = (value - high.astype(jnp.float32)).astype(jnp.bfloat16)
    return high, low


def dot(left, right, contraction):
    return lax.dot_general(
        left, right, (contraction, ((), ())), preferred_element_type=jnp.float32
    )


def dot3(left, right, contraction):
    rows = left[0].shape[0]
    both = dot(jnp.concatenate(left, axis=0), right[0], contraction)
    return both[:rows] + both[rows:] + dot(left[0], right[1], contraction)


NT = ((1,), (1,))
NN = ((1,), (0,))


def factor_kernel(
    sizes, x_hbm, w_hbm, cf_ref, lab_ref, out_hbm, nc_out,
    xs, ws, other, gram, gram_in, gram_row, nc, part, field, left, right, weight, first, second, done,
    load_sem, e_send, e_recv, g_send, g_recv, z_send, z_recv, n_send, n_recv,
    t_send, t_recv, c_send, c_recv, r_send, r_recv, out_sem,
):
    n_row, n_col, n_ch = sizes
    rank, rows, cols = w_hbm.shape
    chans = x_hbm.shape[0]
    share = rank // n_col
    chunks = rows // CHUNK
    early = rows - EDGE * CHUNK
    wide = cols + LANES
    me_row, me_col, me_ch = (lax.axis_index(a) for a in ("row", "col", "ch"))

    halves = cols // LANES
    groups = rows // SUB

    def load(g):
        for h in range(halves):
            for j, (source, target) in enumerate(((w_hbm, ws), (x_hbm, xs))):
                at = (slice(None), pl.ds(g * SUB, SUB))
                yield pltpu.make_async_copy(
                    source.at[at + (pl.ds(h * LANES, LANES),)],
                    target.at[(h,) + at + (slice(None),)],
                    load_sem.at[j, h, g],
                )

    def image_row(buffer, r):
        _, depth, tall, _ = buffer.shape
        return jnp.concatenate(
            [
                buffer.at[h].reshape(depth * tall, LANES)[pl.ds(r, depth, stride=tall), :]
                for h in range(halves)
            ],
            axis=1,
        )

    order = tuple(range(groups - 1, -1, -1))
    for g in order:
        for copy in load(g):
            copy.start()

    barrier = pltpu.get_barrier_semaphore()
    for d in range(1, n_row):
        pl.semaphore_signal(
            barrier, inc=1, device_id={"row": lax.rem(me_row + d, n_row)}, device_id_type=MESH
        )
    for d in range(1, n_col * n_ch):
        pl.semaphore_signal(
            barrier, inc=1, device_id=side(me_col, me_ch, d, n_col, n_ch), device_id_type=MESH
        )

    for buffer in (left, right):
        edge = 0 if buffer is left else n_col - 1

        @pl.when(me_col == edge)
        def _():
            buffer[...] = jnp.zeros_like(buffer)

    for at, edge in ((0, 0), (rows + SMOOTH, n_row - 1)):

        @pl.when(me_row == edge)
        def _():
            field[pl.ds(at, SMOOTH)] = jnp.zeros((SMOOTH,) + field.shape[1:], jnp.float32)

    def marks(r, carry):
        row = (lab_ref[pl.ds(r, 1), :] + 1).astype(jnp.float32)
        field[r + SMOOTH, pl.ds(rank, SUB), pl.ds(0, cols)] = jnp.broadcast_to(row, (SUB, cols))
        return carry

    lax.fori_loop(0, rows, marks, 0)

    gram[...] = jnp.zeros_like(gram)

    def to_early(d):
        return pltpu.make_async_remote_copy(
            xs.at[:, :, pl.ds(early, rows - early), :],
            other.at[d - 1, :, :, pl.ds(early - rows + SUB, rows - early), :],
            e_send.at[d - 1], e_recv.at[d - 1],
            device_id={"ch": lax.rem(me_ch + d, n_ch)}, device_id_type=MESH,
        )

    for i, g in enumerate(order):
        for copy in load(g):
            copy.wait()
        if i == 0:
            pl.semaphore_wait(barrier, n_row - 1 + n_col * n_ch - 1)
            for d in range(1, n_ch):
                to_early(d).start()
        for r in range(g * SUB, g * SUB + SUB):
            both = jnp.concatenate([image_row(ws, r), image_row(xs, r)], axis=0)
            high, low = split(both)
            total = dot3((high[:rank], low[:rank]), (high, low), NT)
            gram[...] += total.reshape(gram.shape)

    def to_col(d):
        peer = lax.rem(me_col + d, n_col)
        return pltpu.make_async_remote_copy(
            gram.at[peer], gram_in.at[d - 1], g_send.at[d - 1], g_recv.at[d - 1],
            device_id={"col": peer}, device_id_type=MESH,
        )

    for d in range(1, n_col):
        to_col(d).start()
    own = gram[me_col]
    for d in range(1, n_col):
        to_col(d).wait_recv()
        own = own + gram_in[d - 1]
    gram_row[me_row] = own

    def to_row(d):
        peer = lax.rem(me_row + d, n_row)
        return pltpu.make_async_remote_copy(
            gram_row.at[me_row], gram_row.at[me_row], z_send.at[d - 1], z_recv.at[d - 1],
            device_id={"row": peer}, device_id_type=MESH,
        )

    def from_row(d):
        peer = lax.rem(me_row + n_row - d, n_row)
        return pltpu.make_async_remote_copy(
            gram_row.at[peer], gram_row.at[peer], z_send.at[d - 1], z_recv.at[d - 1],
            device_id={"row": peer}, device_id_type=MESH,
        )

    for d in range(1, n_row):
        to_row(d).start()
    for d in range(1, n_row):
        from_row(d).wait_recv()
    total = gram_row[0]
    for z in range(1, n_row):
        total = total + gram_row[z]
    lower = jnp.dot(
        total[:, :rank], cf_ref[...], precision=lax.Precision.HIGHEST,
        preferred_element_type=jnp.float32,
    )
    own_cf = cf_ref[pl.ds(pl.multiple_of(me_col * share, share), share), :]
    nc[me_ch, me_col] = own_cf * total[:, rank:] / (lower + epsilon)

    def to_side(d):
        return pltpu.make_async_remote_copy(
            nc.at[me_ch, me_col], nc.at[me_ch, me_col], n_send.at[d - 1], n_recv.at[d - 1],
            device_id=side(me_col, me_ch, d, n_col, n_ch), device_id_type=MESH,
        )

    def from_side(d):
        at = side(me_col, me_ch, n_col * n_ch - d, n_col, n_ch)
        slot = nc.at[at["ch"], at["col"]]
        return pltpu.make_async_remote_copy(
            slot, slot, n_send.at[d - 1], n_recv.at[d - 1],
            device_id=at, device_id_type=MESH,
        )

    for d in range(1, n_col * n_ch):
        to_side(d).start()
    for d in range(1, n_col * n_ch):
        from_side(d).wait_recv()

    mine = nc[me_ch].reshape(rank, chans)
    nc_out[...] = mine
    mine = split(mine)

    def chunk_of(i):
        return lax.rem(i + chunks - EDGE, chunks)

    def to_ch(d, c):
        peer = lax.rem(me_ch + d, n_ch)
        slot = part.at[me_ch, pl.ds(c * CHUNK, CHUNK)]
        return pltpu.make_async_remote_copy(
            slot, slot, t_send.at[d - 1, c], t_recv.at[d - 1, c],
            device_id={"ch": peer}, device_id_type=MESH,
        )

    def from_ch(d, c):
        peer = lax.rem(me_ch + n_ch - d, n_ch)
        slot = part.at[peer, pl.ds(c * CHUNK, CHUNK)]
        return pltpu.make_async_remote_copy(
            slot, slot, t_send.at[d - 1, c], t_recv.at[d - 1, c],
            device_id={"ch": peer}, device_id_type=MESH,
        )

    def send_part(i, carry):
        c = chunk_of(i)
        for k in range(CHUNK):
            r = c * CHUNK + k
            part[me_ch, r] = dot3(mine, split(image_row(xs, r)), NN)
        for d in range(1, n_ch):
            to_ch(d, c).start()
        return carry

    lax.fori_loop(EDGE, chunks, send_part, 0)

    for r in range(early, rows):
        part[me_ch, r] = dot3(mine, split(image_row(xs, r)), NN)
    for d in range(1, n_ch):
        peer = lax.rem(me_ch + n_ch - d, n_ch)
        theirs = split(nc[peer].reshape(rank, chans))
        to_early(d).wait_recv()
        for r in range(early, rows):
            part[peer, r] = dot3(theirs, split(image_row(other.at[d - 1], r - rows + SUB)), NN)

    cg = jnp.zeros((rank, rank), jnp.float32)
    for h in range(n_ch):
        block = nc[h].reshape(rank, chans)
        cg = cg + lax.dot_general(
            block, block, (NT, ((), ())), precision=lax.Precision.HIGHEST,
            preferred_element_type=jnp.float32,
        )
    cg = split(cg)

    def to_right(c):
        return pltpu.make_async_remote_copy(
            field.at[pl.ds(c * CHUNK + SMOOTH, CHUNK), :, pl.ds(cols - LANES, LANES)],
            left.at[pl.ds(c * CHUNK, CHUNK)], c_send.at[0, c], c_recv.at[0, c],
            device_id={"col": lax.rem(me_col + 1, n_col)}, device_id_type=MESH,
        )

    def to_left(c):
        return pltpu.make_async_remote_copy(
            field.at[pl.ds(c * CHUNK + SMOOTH, CHUNK), :, pl.ds(0, LANES)],
            right.at[pl.ds(c * CHUNK, CHUNK)], c_send.at[1, c], c_recv.at[1, c],
            device_id={"col": lax.rem(me_col + n_col - 1, n_col)}, device_id_type=MESH,
        )

    def raise_chunk(i, awaited=True):
        c = chunk_of(i)
        if awaited:
            for d in range(1, n_ch):
                from_ch(d, c).wait_recv()
        for k in range(CHUNK):
            r = c * CHUNK + k
            w = image_row(ws, r)
            top = part[0, r]
            for h in range(1, n_ch):
                top = top + part[h, r]
            low = dot3(cg, split(w), NN)
            field[r + SMOOTH, pl.ds(0, rank), pl.ds(0, cols)] = w * top / (low + epsilon)

        @pl.when(me_col < n_col - 1)
        def _():
            to_right(c).start()

        @pl.when(me_col > 0)
        def _():
            to_left(c).start()

    lane = lax.broadcasted_iota(jnp.int32, (CHUNK, rank + SUB, LANES), 2)

    def widen_chunk(i):
        c = chunk_of(i)

        @pl.when(me_col > 0)
        def _():
            to_right(c).wait_recv()

        @pl.when(me_col < n_col - 1)
        def _():
            to_left(c).wait_recv()

        from_right = jnp.where(lane < SMOOTH, right[pl.ds(c * CHUNK, CHUNK)], 0.0)
        wide = jnp.where(lane >= LANES - SMOOTH, left[pl.ds(c * CHUNK, CHUNK)], from_right)
        field[pl.ds(c * CHUNK + SMOOTH, CHUNK), :, pl.ds(cols, LANES)] = wide

    def to_down():
        return pltpu.make_async_remote_copy(
            field.at[pl.ds(rows, SMOOTH)], field.at[pl.ds(0, SMOOTH)], r_send.at[0], r_recv.at[0],
            device_id={"row": lax.rem(me_row + 1, n_row)}, device_id_type=MESH,
        )

    def to_up():
        return pltpu.make_async_remote_copy(
            field.at[pl.ds(SMOOTH, SMOOTH)], field.at[pl.ds(rows + SMOOTH, SMOOTH)],
            r_send.at[1], r_recv.at[1],
            device_id={"row": lax.rem(me_row + n_row - 1, n_row)}, device_id_type=MESH,
        )

    def coefficients(e):
        center = field[e, pl.ds(rank, SUB), :]
        around = (
            field[e - 1, pl.ds(rank, SUB), :],
            field[e + 1, pl.ds(rank, SUB), :],
            pltpu.roll(center, 1, 1),
            pltpu.roll(center, wide - 1, 1),
        )
        parts = [
            jnp.where(near == 0, 0.0, jnp.where(near == center, 1.0, 0.25)) for near in around
        ]
        scale = 1.0 / (1.0 + parts[0] + parts[1] + parts[2] + parts[3])
        weight[e, 0] = scale
        for j in range(4):
            weight[e, j + 1] = parts[j] * scale

    def smooth(source, e):
        here, up, down = (
            source[at, pl.ds(0, rank), :].reshape(rank // SUB, SUB, wide)
            for at in (e, e - 1, e + 1)
        )
        total = weight[e, 0] * here + weight[e, 1] * up + weight[e, 2] * down
        total = total + weight[e, 3] * pltpu.roll(here, 1, 2)
        total = total + weight[e, 4] * pltpu.roll(here, wide - 1, 2)
        return total.reshape(rank, wide)

    def put(r):
        return pltpu.make_async_copy(done.at[r], out_hbm.at[:, r, :], out_sem.at[r])

    def one(e, carry):
        coefficients(e)
        first[e] = smooth(field, e)
        return carry

    def two(e, carry):
        second[e] = smooth(first, e)
        return carry

    def three(e, carry):
        done[e - SMOOTH] = smooth(second, e)[:, :cols]
        put(e - SMOOTH).start()
        return carry

    def sweep(starts, counts):
        for stage, start, count in zip((one, two, three), starts, counts):
            lax.fori_loop(0, count, lambda k, v, f=stage, s=start: f(s + k, v), 0)

    def sweep_chunk(c):
        sweep((CHUNK * c + 2, CHUNK * c + 1, CHUNK * c), (CHUNK,) * 3)

    for i in range(2 * EDGE):
        raise_chunk(i, awaited=i >= EDGE)
    for i in range(2 * EDGE):
        widen_chunk(i)

    @pl.when(me_row < n_row - 1)
    def _():
        to_down().start()

    @pl.when(me_row > 0)
    def _():
        to_up().start()

    for i in range(2 * EDGE, 2 * EDGE + LAG):
        raise_chunk(i)
        if i > 2 * EDGE:
            widen_chunk(i - 1)

    @pl.when(me_row > 0)
    def _():
        to_down().wait_recv()

    @pl.when(me_row < n_row - 1)
    def _():
        to_up().wait_recv()

    tip = CHUNK * EDGE
    sweep((1, 2, 3), (tip + 1, tip - 1, tip - 3))
    for c in range(EDGE, EDGE + LAG - 1):
        sweep_chunk(c)

    def step(i, carry):
        raise_chunk(i)
        widen_chunk(i - 1)
        sweep_chunk(i - 1 - EDGE)
        return carry

    lax.fori_loop(2 * EDGE + LAG, chunks, step, 0)
    widen_chunk(chunks - 1)
    sweep_chunk(chunks - 1 - EDGE)
    sweep((early + 2, early + 1, early), (tip + 3,) * 3)

    for d in range(1, n_col):
        to_col(d).wait_send()
    for d in range(1, n_row):
        to_row(d).wait_send()
    for d in range(1, n_col * n_ch):
        to_side(d).wait_send()

    def drain(c, carry):
        @pl.when(me_col < n_col - 1)
        def _():
            to_right(c).wait_send()

        @pl.when(me_col > 0)
        def _():
            to_left(c).wait_send()

        return carry

    lax.fori_loop(0, chunks, drain, 0)

    def drain_part(i, carry):
        for d in range(1, n_ch):
            to_ch(d, chunk_of(i)).wait_send()
        return carry

    lax.fori_loop(EDGE, chunks, drain_part, 0)
    for d in range(1, n_ch):
        to_early(d).wait_send()

    @pl.when(me_row < n_row - 1)
    def _():
        to_down().wait_send()

    @pl.when(me_row > 0)
    def _():
        to_up().wait_send()

    def drain_out(r, carry):
        put(r).wait()
        return carry

    lax.fori_loop(0, rows, drain_out, 0)


def side(me_col, me_ch, d, n_col, n_ch):
    place = lax.rem(me_col * n_ch + me_ch + d, n_col * n_ch)
    return {"col": place // n_ch, "ch": lax.rem(place, n_ch)}


def shards(sizes, spectra, pixel_factor, channel_factor, labels):
    n_row, n_col, n_ch = sizes
    rank, rows, cols = pixel_factor.shape
    chans = spectra.shape[0]
    share = rank // n_col
    chunks = rows // CHUNK
    tall = rows + 2 * SMOOTH
    wide = cols + LANES
    f32 = jnp.float32
    vmem = pl.BlockSpec(memory_space=pltpu.VMEM)
    anywhere = pl.BlockSpec(memory_space=pl.ANY)
    dma = pltpu.SemaphoreType.DMA
    return pl.pallas_call(
        functools.partial(factor_kernel, sizes),
        out_shape=(
            jax.ShapeDtypeStruct(pixel_factor.shape, f32),
            jax.ShapeDtypeStruct(channel_factor.shape, f32),
        ),
        in_specs=[anywhere, anywhere, vmem, vmem],
        out_specs=(anywhere, vmem),
        scratch_shapes=[
            pltpu.VMEM((cols // LANES, chans, rows, LANES), f32),
            pltpu.VMEM((cols // LANES, rank, rows, LANES), f32),
            pltpu.VMEM((n_ch - 1, cols // LANES, chans, SUB, LANES), f32),
            pltpu.VMEM((n_col, share, rank + chans), f32),
            pltpu.VMEM((n_col - 1, share, rank + chans), f32),
            pltpu.VMEM((n_row, share, rank + chans), f32),
            pltpu.VMEM((n_ch, n_col, share, chans), f32),
            pltpu.VMEM((n_ch, rows, rank, cols), f32),
            pltpu.VMEM((tall, rank + SUB, wide), f32),
            pltpu.VMEM((rows, rank + SUB, LANES), f32),
            pltpu.VMEM((rows, rank + SUB, LANES), f32),
            pltpu.VMEM((tall, 5, SUB, wide), f32),
            pltpu.VMEM((tall, rank, wide), f32),
            pltpu.VMEM((tall, rank, wide), f32),
            pltpu.VMEM((rows, rank, cols), f32),
            dma((2, cols // LANES, rows // SUB)),
            dma((n_ch - 1,)), dma((n_ch - 1,)),
            dma((n_col - 1,)), dma((n_col - 1,)),
            dma((n_row - 1,)), dma((n_row - 1,)),
            dma((n_col * n_ch - 1,)), dma((n_col * n_ch - 1,)),
            dma((n_ch - 1, chunks)), dma((n_ch - 1, chunks)),
            dma((2, chunks)), dma((2, chunks)),
            dma((2,)), dma((2,)),
            dma((rows,)),
        ],
        compiler_params=pltpu.CompilerParams(
            collective_id=0, has_side_effects=True, vmem_limit_bytes=60 * 1024 * 1024
        ),
        name="factor",
    )(spectra, pixel_factor, channel_factor, labels)


def solution(mesh):
    sizes = tuple(mesh.shape[a] for a in ("row", "col", "ch"))
    placed = (P("ch", "row", "col"), P(None, "row", "col"), P(None, "ch"), P("row", "col"))
    return jax.shard_map(
        functools.partial(shards, sizes),
        mesh=mesh,
        in_specs=placed,
        out_specs=(P(None, "row", "col"), P(None, "ch")),
        check_vma=False,
    )
```

```python
import functools

import jax
import jax.numpy as jnp
from jax import lax
from jax.experimental import pallas as pl
from jax.experimental.pallas import tpu as pltpu
from jax.sharding import PartitionSpec as P

SMOOTH = 3
MESH = pl.DeviceIdType.MESH
LANES = 128
SUB = 8
CHUNK = 2
EDGE = -(-SMOOTH // CHUNK)
LAG = 4

epsilon = 1e-09


def split(value):
    high = value.astype(jnp.bfloat16)
    low = (value - high.astype(jnp.float32)).astype(jnp.bfloat16)
    return high, low


def dot(left, right, contraction):
    return lax.dot_general(
        left, right, (contraction, ((), ())), preferred_element_type=jnp.float32
    )


def dot3(left, right, contraction):
    rows = left[0].shape[0]
    both = dot(jnp.concatenate(left, axis=0), right[0], contraction)
    return both[:rows] + both[rows:] + dot(left[0], right[1], contraction)


NT = ((1,), (1,))
NN = ((1,), (0,))


def factor_kernel(
    sizes, x_hbm, w_hbm, cf_ref, lab_ref, out_hbm, nc_out,
    xs, ws, other, gram, gram_in, gram_row, nc, part, field, left, right, weight, first, second, done,
    load_sem, e_send, e_recv, g_send, g_recv, z_send, z_recv, n_send, n_recv,
    t_send, t_recv, c_send, c_recv, r_send, r_recv, out_sem,
):
    n_row, n_col, n_ch = sizes
    rank, rows, cols = w_hbm.shape
    chans = x_hbm.shape[0]
    share = rank // n_col
    chunks = rows // CHUNK
    early = rows - EDGE * CHUNK
    wide = cols + LANES
    me_row, me_col, me_ch = (lax.axis_index(a) for a in ("row", "col", "ch"))

    halves = cols // LANES
    groups = rows // SUB

    def load(g):
        for h in range(halves):
            for j, (source, target) in enumerate(((w_hbm, ws), (x_hbm, xs))):
                at = (slice(None), pl.ds(g * SUB, SUB))
                yield pltpu.make_async_copy(
                    source.at[at + (pl.ds(h * LANES, LANES),)],
                    target.at[(h,) + at + (slice(None),)],
                    load_sem.at[j, h, g],
                )

    def image_row(buffer, r):
        _, depth, tall, _ = buffer.shape
        return jnp.concatenate(
            [
                buffer.at[h].reshape(depth * tall, LANES)[pl.ds(r, depth, stride=tall), :]
                for h in range(halves)
            ],
            axis=1,
        )

    order = tuple(range(groups - 1, -1, -1))
    for g in order:
        for copy in load(g):
            copy.start()

    barrier = pltpu.get_barrier_semaphore()
    for d in range(1, n_row):
        pl.semaphore_signal(
            barrier, inc=1, device_id={"row": lax.rem(me_row + d, n_row)}, device_id_type=MESH
        )
    for d in range(1, n_col * n_ch):
        pl.semaphore_signal(
            barrier, inc=1, device_id=side(me_col, me_ch, d, n_col, n_ch), device_id_type=MESH
        )

    for buffer in (left, right):
        edge = 0 if buffer is left else n_col - 1

        @pl.when(me_col == edge)
        def _():
            buffer[...] = jnp.zeros_like(buffer)

    for at, edge in ((0, 0), (rows + SMOOTH, n_row - 1)):

        @pl.when(me_row == edge)
        def _():
            field[pl.ds(at, SMOOTH)] = jnp.zeros((SMOOTH,) + field.shape[1:], jnp.float32)

    def marks(r, carry):
        row = (lab_ref[pl.ds(r, 1), :] + 1).astype(jnp.float32)
        field[r + SMOOTH, pl.ds(rank, SUB), pl.ds(0, cols)] = jnp.broadcast_to(row, (SUB, cols))
        return carry

    lax.fori_loop(0, rows, marks, 0)

    gram[...] = jnp.zeros_like(gram)

    def to_early(d):
        return pltpu.make_async_remote_copy(
            xs.at[:, :, pl.ds(early, rows - early), :],
            other.at[d - 1, :, :, pl.ds(early - rows + SUB, rows - early), :],
            e_send.at[d - 1], e_recv.at[d - 1],
            device_id={"ch": lax.rem(me_ch + d, n_ch)}, device_id_type=MESH,
        )

    for i, g in enumerate(order):
        for copy in load(g):
            copy.wait()
        if i == 0:
            pl.semaphore_wait(barrier, n_row - 1 + n_col * n_ch - 1)
            for d in range(1, n_ch):
                to_early(d).start()
        for r in range(g * SUB, g * SUB + SUB):
            both = jnp.concatenate([image_row(ws, r), image_row(xs, r)], axis=0)
            high, low = split(both)
            total = dot3((high[:rank], low[:rank]), (high, low), NT)
            gram[...] += total.reshape(gram.shape)

    def to_col(d):
        peer = lax.rem(me_col + d, n_col)
        return pltpu.make_async_remote_copy(
            gram.at[peer], gram_in.at[d - 1], g_send.at[d - 1], g_recv.at[d - 1],
            device_id={"col": peer}, device_id_type=MESH,
        )

    for d in range(1, n_col):
        to_col(d).start()
    own = gram[me_col]
    for d in range(1, n_col):
        to_col(d).wait_recv()
        own = own + gram_in[d - 1]
    gram_row[me_row] = own

    def to_row(d):
        peer = lax.rem(me_row + d, n_row)
        return pltpu.make_async_remote_copy(
            gram_row.at[me_row], gram_row.at[me_row], z_send.at[d - 1], z_recv.at[d - 1],
            device_id={"row": peer}, device_id_type=MESH,
        )

    def from_row(d):
        peer = lax.rem(me_row + n_row - d, n_row)
        return pltpu.make_async_remote_copy(
            gram_row.at[peer], gram_row.at[peer], z_send.at[d - 1], z_recv.at[d - 1],
            device_id={"row": peer}, device_id_type=MESH,
        )

    for d in range(1, n_row):
        to_row(d).start()
    for d in range(1, n_row):
        from_row(d).wait_recv()
    total = gram_row[0]
    for z in range(1, n_row):
        total = total + gram_row[z]
    lower = jnp.dot(
        total[:, :rank], cf_ref[...], precision=lax.Precision.HIGHEST,
        preferred_element_type=jnp.float32,
    )
    own_cf = cf_ref[pl.ds(pl.multiple_of(me_col * share, share), share), :]
    nc[me_ch, me_col] = own_cf * total[:, rank:] / (lower + epsilon)

    def to_side(d):
        return pltpu.make_async_remote_copy(
            nc.at[me_ch, me_col], nc.at[me_ch, me_col], n_send.at[d - 1], n_recv.at[d - 1],
            device_id=side(me_col, me_ch, d, n_col, n_ch), device_id_type=MESH,
        )

    def from_side(d):
        at = side(me_col, me_ch, n_col * n_ch - d, n_col, n_ch)
        slot = nc.at[at["ch"], at["col"]]
        return pltpu.make_async_remote_copy(
            slot, slot, n_send.at[d - 1], n_recv.at[d - 1],
            device_id=at, device_id_type=MESH,
        )

    for d in range(1, n_col * n_ch):
        to_side(d).start()
    for d in range(1, n_col * n_ch):
        from_side(d).wait_recv()

    mine = nc[me_ch].reshape(rank, chans)
    nc_out[...] = mine
    mine = split(mine)

    def chunk_of(i):
        return lax.rem(i + chunks - EDGE, chunks)

    def to_ch(d, c):
        peer = lax.rem(me_ch + d, n_ch)
        slot = part.at[me_ch, pl.ds(c * CHUNK, CHUNK)]
        return pltpu.make_async_remote_copy(
            slot, slot, t_send.at[d - 1, c], t_recv.at[d - 1, c],
            device_id={"ch": peer}, device_id_type=MESH,
        )

    def from_ch(d, c):
        peer = lax.rem(me_ch + n_ch - d, n_ch)
        slot = part.at[peer, pl.ds(c * CHUNK, CHUNK)]
        return pltpu.make_async_remote_copy(
            slot, slot, t_send.at[d - 1, c], t_recv.at[d - 1, c],
            device_id={"ch": peer}, device_id_type=MESH,
        )

    def send_part(i, carry):
        c = chunk_of(i)
        for k in range(CHUNK):
            r = c * CHUNK + k
            part[me_ch, r] = dot3(mine, split(image_row(xs, r)), NN)
        for d in range(1, n_ch):
            to_ch(d, c).start()
        return carry

    lax.fori_loop(EDGE, chunks, send_part, 0)

    for r in range(early, rows):
        part[me_ch, r] = dot3(mine, split(image_row(xs, r)), NN)
    for d in range(1, n_ch):
        peer = lax.rem(me_ch + n_ch - d, n_ch)
        theirs = split(nc[peer].reshape(rank, chans))
        to_early(d).wait_recv()
        for r in range(early, rows):
            part[peer, r] = dot3(theirs, split(image_row(other.at[d - 1], r - rows + SUB)), NN)

    cg = jnp.zeros((rank, rank), jnp.float32)
    for h in range(n_ch):
        block = nc[h].reshape(rank, chans)
        cg = cg + lax.dot_general(
            block, block, (NT, ((), ())), precision=lax.Precision.HIGHEST,
            preferred_element_type=jnp.float32,
        )
    cg = split(cg)

    def to_right(c):
        return pltpu.make_async_remote_copy(
            field.at[pl.ds(c * CHUNK + SMOOTH, CHUNK), :, pl.ds(cols - LANES, LANES)],
            left.at[pl.ds(c * CHUNK, CHUNK)], c_send.at[0, c], c_recv.at[0, c],
            device_id={"col": lax.rem(me_col + 1, n_col)}, device_id_type=MESH,
        )

    def to_left(c):
        return pltpu.make_async_remote_copy(
            field.at[pl.ds(c * CHUNK + SMOOTH, CHUNK), :, pl.ds(0, LANES)],
            right.at[pl.ds(c * CHUNK, CHUNK)], c_send.at[1, c], c_recv.at[1, c],
            device_id={"col": lax.rem(me_col + n_col - 1, n_col)}, device_id_type=MESH,
        )

    def raise_chunk(i, awaited=True):
        c = chunk_of(i)
        if awaited:
            for d in range(1, n_ch):
                from_ch(d, c).wait_recv()
        for k in range(CHUNK):
            r = c * CHUNK + k
            w = image_row(ws, r)
            top = part[0, r]
            for h in range(1, n_ch):
                top = top + part[h, r]
            low = dot3(cg, split(w), NN)
            field[r + SMOOTH, pl.ds(0, rank), pl.ds(0, cols)] = w * top / (low + epsilon)

        @pl.when(me_col < n_col - 1)
        def _():
            to_right(c).start()

        @pl.when(me_col > 0)
        def _():
            to_left(c).start()

    lane = lax.broadcasted_iota(jnp.int32, (CHUNK, rank + SUB, LANES), 2)

    def widen_chunk(i):
        c = chunk_of(i)

        @pl.when(me_col > 0)
        def _():
            to_right(c).wait_recv()

        @pl.when(me_col < n_col - 1)
        def _():
            to_left(c).wait_recv()

        from_right = jnp.where(lane < SMOOTH, right[pl.ds(c * CHUNK, CHUNK)], 0.0)
        wide = jnp.where(lane >= LANES - SMOOTH, left[pl.ds(c * CHUNK, CHUNK)], from_right)
        field[pl.ds(c * CHUNK + SMOOTH, CHUNK), :, pl.ds(cols, LANES)] = wide

    def to_down():
        return pltpu.make_async_remote_copy(
            field.at[pl.ds(rows, SMOOTH)], field.at[pl.ds(0, SMOOTH)], r_send.at[0], r_recv.at[0],
            device_id={"row": lax.rem(me_row + 1, n_row)}, device_id_type=MESH,
        )

    def to_up():
        return pltpu.make_async_remote_copy(
            field.at[pl.ds(SMOOTH, SMOOTH)], field.at[pl.ds(rows + SMOOTH, SMOOTH)],
            r_send.at[1], r_recv.at[1],
            device_id={"row": lax.rem(me_row + n_row - 1, n_row)}, device_id_type=MESH,
        )

    def coefficients(e):
        center = field[e, pl.ds(rank, SUB), :]
        around = (
            field[e - 1, pl.ds(rank, SUB), :],
            field[e + 1, pl.ds(rank, SUB), :],
            pltpu.roll(center, 1, 1),
            pltpu.roll(center, wide - 1, 1),
        )
        parts = [
            jnp.where(near == 0, 0.0, jnp.where(near == center, 1.0, 0.25)) for near in around
        ]
        scale = 1.0 / (1.0 + parts[0] + parts[1] + parts[2] + parts[3])
        weight[e, 0] = scale
        for j in range(4):
            weight[e, j + 1] = parts[j] * scale

    def smooth(source, e):
        here, up, down = (
            source[at, pl.ds(0, rank), :].reshape(rank // SUB, SUB, wide)
            for at in (e, e - 1, e + 1)
        )
        total = weight[e, 0] * here + weight[e, 1] * up + weight[e, 2] * down
        total = total + weight[e, 3] * pltpu.roll(here, 1, 2)
        total = total + weight[e, 4] * pltpu.roll(here, wide - 1, 2)
        return total.reshape(rank, wide)

    def put(r):
        return pltpu.make_async_copy(done.at[r], out_hbm.at[:, r, :], out_sem.at[r])

    def one(e, carry):
        coefficients(e)
        first[e] = smooth(field, e)
        return carry

    def two(e, carry):
        second[e] = smooth(first, e)
        return carry

    def three(e, carry):
        done[e - SMOOTH] = smooth(second, e)[:, :cols]
        put(e - SMOOTH).start()
        return carry

    def sweep(starts, counts):
        for stage, start, count in zip((one, two, three), starts, counts):
            lax.fori_loop(0, count, lambda k, v, f=stage, s=start: f(s + k, v), 0)

    def sweep_chunk(c):
        sweep((CHUNK * c + 2, CHUNK * c + 1, CHUNK * c), (CHUNK,) * 3)

    for i in range(2 * EDGE):
        raise_chunk(i, awaited=i >= EDGE)
    for i in range(2 * EDGE):
        widen_chunk(i)

    @pl.when(me_row < n_row - 1)
    def _():
        to_down().start()

    @pl.when(me_row > 0)
    def _():
        to_up().start()

    for i in range(2 * EDGE, 2 * EDGE + LAG):
        raise_chunk(i)
        if i > 2 * EDGE + 1:
            widen_chunk(i - 2)

    @pl.when(me_row > 0)
    def _():
        to_down().wait_recv()

    @pl.when(me_row < n_row - 1)
    def _():
        to_up().wait_recv()

    tip = CHUNK * EDGE
    sweep((1, 2, 3), (tip + 1, tip - 1, tip - 3))
    for c in range(EDGE, EDGE + LAG - 2):
        sweep_chunk(c)

    def step(i, carry):
        widen_chunk(i - 2)
        sweep_chunk(i - 2 - EDGE)
        raise_chunk(i)
        return carry

    lax.fori_loop(2 * EDGE + LAG, chunks, step, 0)
    for i in (chunks - 2, chunks - 1):
        widen_chunk(i)
        sweep_chunk(i - EDGE)
    sweep((early + 2, early + 1, early), (tip + 3,) * 3)

    for d in range(1, n_col):
        to_col(d).wait_send()
    for d in range(1, n_row):
        to_row(d).wait_send()
    for d in range(1, n_col * n_ch):
        to_side(d).wait_send()

    def drain(c, carry):
        @pl.when(me_col < n_col - 1)
        def _():
            to_right(c).wait_send()

        @pl.when(me_col > 0)
        def _():
            to_left(c).wait_send()

        return carry

    lax.fori_loop(0, chunks, drain, 0)

    def drain_part(i, carry):
        for d in range(1, n_ch):
            to_ch(d, chunk_of(i)).wait_send()
        return carry

    lax.fori_loop(EDGE, chunks, drain_part, 0)
    for d in range(1, n_ch):
        to_early(d).wait_send()

    @pl.when(me_row < n_row - 1)
    def _():
        to_down().wait_send()

    @pl.when(me_row > 0)
    def _():
        to_up().wait_send()

    def drain_out(r, carry):
        put(r).wait()
        return carry

    lax.fori_loop(0, rows, drain_out, 0)


def side(me_col, me_ch, d, n_col, n_ch):
    place = lax.rem(me_col * n_ch + me_ch + d, n_col * n_ch)
    return {"col": place // n_ch, "ch": lax.rem(place, n_ch)}


def shards(sizes, spectra, pixel_factor, channel_factor, labels):
    n_row, n_col, n_ch = sizes
    rank, rows, cols = pixel_factor.shape
    chans = spectra.shape[0]
    share = rank // n_col
    chunks = rows // CHUNK
    tall = rows + 2 * SMOOTH
    wide = cols + LANES
    f32 = jnp.float32
    vmem = pl.BlockSpec(memory_space=pltpu.VMEM)
    anywhere = pl.BlockSpec(memory_space=pl.ANY)
    dma = pltpu.SemaphoreType.DMA
    return pl.pallas_call(
        functools.partial(factor_kernel, sizes),
        out_shape=(
            jax.ShapeDtypeStruct(pixel_factor.shape, f32),
            jax.ShapeDtypeStruct(channel_factor.shape, f32),
        ),
        in_specs=[anywhere, anywhere, vmem, vmem],
        out_specs=(anywhere, vmem),
        scratch_shapes=[
            pltpu.VMEM((cols // LANES, chans, rows, LANES), f32),
            pltpu.VMEM((cols // LANES, rank, rows, LANES), f32),
            pltpu.VMEM((n_ch - 1, cols // LANES, chans, SUB, LANES), f32),
            pltpu.VMEM((n_col, share, rank + chans), f32),
            pltpu.VMEM((n_col - 1, share, rank + chans), f32),
            pltpu.VMEM((n_row, share, rank + chans), f32),
            pltpu.VMEM((n_ch, n_col, share, chans), f32),
            pltpu.VMEM((n_ch, rows, rank, cols), f32),
            pltpu.VMEM((tall, rank + SUB, wide), f32),
            pltpu.VMEM((rows, rank + SUB, LANES), f32),
            pltpu.VMEM((rows, rank + SUB, LANES), f32),
            pltpu.VMEM((tall, 5, SUB, wide), f32),
            pltpu.VMEM((tall, rank, wide), f32),
            pltpu.VMEM((tall, rank, wide), f32),
            pltpu.VMEM((rows, rank, cols), f32),
            dma((2, cols // LANES, rows // SUB)),
            dma((n_ch - 1,)), dma((n_ch - 1,)),
            dma((n_col - 1,)), dma((n_col - 1,)),
            dma((n_row - 1,)), dma((n_row - 1,)),
            dma((n_col * n_ch - 1,)), dma((n_col * n_ch - 1,)),
            dma((n_ch - 1, chunks)), dma((n_ch - 1, chunks)),
            dma((2, chunks)), dma((2, chunks)),
            dma((2,)), dma((2,)),
            dma((rows,)),
        ],
        compiler_params=pltpu.CompilerParams(
            collective_id=0, has_side_effects=True, vmem_limit_bytes=60 * 1024 * 1024
        ),
        name="factor",
    )(spectra, pixel_factor, channel_factor, labels)


def solution(mesh):
    sizes = tuple(mesh.shape[a] for a in ("row", "col", "ch"))
    placed = (P("ch", "row", "col"), P(None, "row", "col"), P(None, "ch"), P("row", "col"))
    return jax.shard_map(
        functools.partial(shards, sizes),
        mesh=mesh,
        in_specs=placed,
        out_specs=(P(None, "row", "col"), P(None, "ch")),
        check_vma=False,
    )
```
